512 devices in a mesh: sub: 64 (over y, z), grp: 8 (over x, core).
Axes of the slice: x: 4, y: 4, z: 16, core: 2. Of those that a mesh axis runs over, the one named last changes fastest.
Arguments:
- margin_basis: bfloat16 [512, 6, 384, 128], P(('sub', 'grp')), may hold values from -6 to 6
- pair_matrix: bfloat16 [512, 6, 384, 384], P(('sub', 'grp')), as said below
- own_basis: bfloat16 [512, 2048, 128], P(('sub', 'grp')), may hold values from -0.125 to 0.125
- own_image: bfloat16 [512, 2048, 128], P(('sub', 'grp')), may hold values from -6 to 6
- tile_counts: int32 [512, 6], P(('sub', 'grp')), may hold values from 0 to 3, as said below
Outputs:
- coarse_rows: float32 [512, 7, 128, 128], P('sub', None, 'grp')
The draws below stay inside these ranges and needn't reach their ends.
Inputs may be any that keep to these rules, and one draw needn't show every extreme that they name: `tile_counts`: tile counts of the two slots of one neighbour pair are equal, zero for slots without neighbour, and the pairs of subdomains 0 and 1 and of subdomains (31) * 8 and (32) * 8 have 3 tiles in every draw. pair_matrix[s + stride, 2j + 1] is the transpose of pair_matrix[s, 2j] wherever both are neighbours.
All inputs are finite; a program needn't handle non-finite values.
Results may differ from the reference program's by a relative error of at most 0.0026.
Values may be sent and summed in bfloat16 or wider, within the bound.
No kernel may reach another device: no remote copies, remote signals or barrier semaphores. Data moves between devices by JAX's collectives and lax.ppermute only.
A program may use at most 64 MiB of HBM per device.

```python
import jax
import jax.numpy as jnp

EIG = 128
ROW_TILE = 128
PAIR_TILES = 3
SPAN = 8
OWN_ROWS = 2048
GROUP = 8
LINES = 64
SUBS = 512
PAIR_ROWS = 384


def draw_tile_counts(key, part):
    index = jnp.arange(SUBS, dtype=jnp.int32)
    coord_x = index % GROUP
    plane = index // GROUP
    upper_tiles = jax.random.randint(jax.random.fold_in(key, 11), (SUBS, 3), 0, PAIR_TILES + 1)
    upper_tiles = upper_tiles.at[0, 0].set(PAIR_TILES)
    upper_tiles = upper_tiles.at[(LINES // 2 - 1) * GROUP, 1].set(PAIR_TILES)
    inside = (coord_x + 1 < GROUP, plane + 1 < LINES, plane + SPAN < LINES)
    below = (coord_x >= 1, plane >= 1, plane >= SPAN)
    columns = []
    for which, stride in enumerate((1, GROUP, SPAN * GROUP)):
        upper = jnp.where(inside[which], upper_tiles[:, which], 0)
        lower = jnp.where(below[which], jnp.roll(upper, stride), 0)
        columns.append(upper)
        columns.append(lower)
    return jnp.stack(columns, axis=1).astype(jnp.int32)


def draw_pair_matrix(key, part):
    shape = (SUBS, 3, PAIR_ROWS, PAIR_ROWS)
    base = jax.random.normal(jax.random.fold_in(key, 21), shape)
    base = (base / PAIR_ROWS).astype(jnp.bfloat16)
    blocks = []
    for which, stride in enumerate((1, GROUP, SPAN * GROUP)):
        upper = base[:, which]
        blocks.append(upper)
        blocks.append(jnp.swapaxes(jnp.roll(upper, stride, axis=0), 1, 2))
    return jnp.stack(blocks, axis=1)


def levels(stream_key, shape, pieces, smallest, high):
    def one(position, blocks):
        heights = jax.random.uniform(jax.random.fold_in(jax.random.fold_in(stream_key, 6), position), (blocks,), jnp.float32, smallest / len(pieces), high / len(pieces))
        return jnp.repeat(jnp.exp(heights), shape[position] // blocks).reshape((-1,) + (1,) * (len(shape) - position - 1))

    gain = one(*pieces[0])
    for cut in pieces[1:]:
        gain = gain * one(*cut)
    return gain


def normal_values(key, shape, spread, most, split=(), held_as=jnp.bfloat16):
    values = spread * jax.random.normal(key, shape, jnp.float32)
    if split:
        values = values * levels(key, shape, split, -0.22, 0.18)
    return jnp.clip(values, -most, most).astype(held_as)


def setup_inputs(seed: int = 0) -> dict:
    key_list = jax.random.split(jax.random.key(seed), 6)
    margin_basis = normal_values(key_list[0], (SUBS, 6, PAIR_ROWS, EIG), 1.0, 6.0, ((0, 512),))
    pair_matrix = draw_pair_matrix(jax.random.fold_in(key_list[5], 71), 0)
    own_basis = normal_values(key_list[2], (SUBS, OWN_ROWS, EIG), OWN_ROWS ** -0.5, 0.125, ((0, 512),))
    own_image = normal_values(key_list[3], (SUBS, OWN_ROWS, EIG), 1.0, 6.0, ((0, 512),))
    tile_counts = draw_tile_counts(jax.random.fold_in(key_list[5], 71), 0)
    return dict(margin_basis=margin_basis, pair_matrix=pair_matrix, own_basis=own_basis, own_image=own_image, tile_counts=tile_counts)


def reference(margin_basis, pair_matrix, own_basis, own_image, tile_counts):
    single = jnp.float32
    diagonal_block = jnp.einsum('sre,srf->sef', own_basis.astype(single), own_image.astype(single))
    row_index = jnp.arange(PAIR_ROWS, dtype=jnp.int32)
    live_rows = row_index[None, None, :, None] < tile_counts[:, :, None, None] * ROW_TILE
    masked_basis = jnp.where(live_rows, margin_basis, jnp.zeros((), jnp.bfloat16))
    blocks = [diagonal_block, None, None, None, None, None, None]
    for which, stride in enumerate((1, GROUP, SPAN * GROUP)):
        upper = 2 * which
        lower = upper + 1
        partner = jnp.roll(masked_basis[:, lower], -stride, axis=0)
        applied = jnp.einsum('src,sce->sre', pair_matrix[:, upper].astype(single), partner.astype(single)).astype(jnp.bfloat16)
        coupling = jnp.einsum('sre,srf->sef', masked_basis[:, upper].astype(single), applied.astype(single))
        blocks[1 + upper] = coupling
        blocks[1 + lower] = jnp.roll(jnp.swapaxes(coupling, 1, 2), stride, axis=0)
    return jnp.stack(blocks, axis=1)
```

```python
import jax
import jax.numpy as jnp
from jax import lax
from jax.experimental import pallas as pl
from jax.experimental.pallas import tpu as pltpu
from jax.sharding import PartitionSpec as P


ROW_TILE = 128
SPAN = 8
EIG = 128
ROWS = 384
SHARE = 16


def shifted(value, axis, steps):
    count = lax.axis_size(axis)
    initial, last = (max(0, -steps), min(count, count - steps))
    return lax.ppermute(value, axis, [(source, source + steps) for source in range(initial, last)])


def masked(block, tile_count):
    row_index = lax.broadcasted_iota(jnp.int32, block.shape, 0)
    return jnp.where(row_index < tile_count * ROW_TILE, block, jnp.zeros((), block.dtype))


def contract_rows(left, right):
    return lax.dot_general(
        left, right, (((0,), (0,)), ((), ())), preferred_element_type=jnp.float32
    )


def upper_block(basis, matrix, received, count):
    image = jnp.dot(matrix, masked(received, count), preferred_element_type=jnp.float32)
    return contract_rows(masked(basis, count), image.astype(jnp.bfloat16))


def lower_left(basis, matrix, count):
    return contract_rows(masked(basis, count), matrix).astype(jnp.bfloat16)


def lower_block(left, received, count):
    return jnp.dot(left, masked(received, count), preferred_element_type=jnp.float32)


def shares(block):
    return block.astype(jnp.bfloat16).reshape(EIG // SHARE, SHARE, EIG)


def near_kernel(counts, margin, matrices, own_basis, own_image, x_above, y_above, y_below, out, z_left):
    z_left[...] = lower_left(margin[0, 5], matrices[0, 5], counts[0, 5])
    out[:, 0] = shares(contract_rows(own_basis[0], own_image[0]))
    along_x = upper_block(margin[0, 0], matrices[0, 0], x_above[...], counts[0, 0])
    out[:, 1] = shares(along_x)
    out[:, 2] = shares(along_x.T)
    out[:, 3] = shares(upper_block(margin[0, 2], matrices[0, 2], y_above[...], counts[0, 2]))
    left = lower_left(margin[0, 3], matrices[0, 3], counts[0, 3])
    out[:, 4] = shares(lower_block(left, y_below[...], counts[0, 3]))


def far_kernel(counts, margin, matrix, left, z_above, z_below, near, out):
    out[:, :5] = near[...]
    out[:, 5] = shares(upper_block(margin[0, 0], matrix[0, 0], z_above[...], counts[0, 4]))
    out[:, 6] = shares(lower_block(left[...], z_below[...], counts[0, 5]))


def spread_kernel(rows, out):
    out[:, :2] = rows[:, :2].astype(jnp.float32)
    out[0, 2] = jnp.zeros((SHARE, EIG), jnp.float32)
    out[1:, 2] = rows[:-1, 2].astype(jnp.float32)
    out[:, 3:] = rows[:, 3:].astype(jnp.float32)


def on_chip(value):
    return pltpu.with_memory_space_constraint(value, pltpu.VMEM)


def local(margin_basis, pair_matrix, own_basis, own_image, tile_counts):
    smem = pl.BlockSpec(memory_space=pltpu.SMEM)
    vmem = pl.BlockSpec(memory_space=pltpu.VMEM)
    far_up, far_down = margin_basis[0, 5], margin_basis[0, 4]
    far_up, far_down, margin = lax.optimization_barrier((far_up, far_down, margin_basis))
    z_above = shifted(far_up, "sub", -SPAN)
    z_below = shifted(far_down, "sub", SPAN)
    x_above = shifted(margin[0, 1], "grp", -1)
    y_above = shifted(margin[0, 3], "sub", -1)
    y_below = shifted(margin[0, 2], "sub", 1)
    near, z_left = pl.pallas_call(
        near_kernel,
        out_shape=(
            pltpu.VMEM((8, 5, SHARE, EIG), jnp.bfloat16),
            pltpu.VMEM((EIG, ROWS), jnp.bfloat16),
        ),
        in_specs=[smem] + [vmem] * 7,
        out_specs=(vmem, vmem),
    )(
        tile_counts,
        margin_basis,
        pair_matrix,
        own_basis,
        own_image,
        on_chip(x_above),
        on_chip(y_above),
        on_chip(y_below),
    )
    coarse = pl.pallas_call(
        far_kernel,
        grid=(1,),
        out_shape=pltpu.VMEM((8, 7, SHARE, EIG), jnp.bfloat16),
        in_specs=[
            smem,
            pl.BlockSpec((1, 1, ROWS, EIG), lambda i: (0, 4, 0, 0)),
            pl.BlockSpec((1, 1, ROWS, ROWS), lambda i: (0, 4, 0, 0)),
            vmem,
            vmem,
            vmem,
            vmem,
        ],
        out_specs=vmem,
    )(
        tile_counts,
        margin_basis,
        pair_matrix,
        on_chip(z_left),
        on_chip(z_above),
        on_chip(z_below),
        on_chip(near),
    )
    rows = lax.all_to_all(coarse, "grp", split_axis=0, concat_axis=0, tiled=True)
    return pl.pallas_call(
        spread_kernel,
        out_shape=jax.ShapeDtypeStruct((8, 7, SHARE, EIG), jnp.float32),
        in_specs=[vmem],
        out_specs=vmem,
    )(on_chip(rows))


def solution(mesh):
    return jax.shard_map(
        local,
        mesh=mesh,
        in_specs=(
            P(("sub", "grp"), None, None, None),
            P(("sub", "grp"), None, None, None),
            P(("sub", "grp"), None, None),
            P(("sub", "grp"), None, None),
            P(("sub", "grp"), None),
        ),
        out_specs=P("sub", None, "grp", None),
        check_vma=False,
    )
```

```python
import jax
import jax.numpy as jnp
from jax import lax
from jax.experimental import pallas as pl
from jax.experimental.pallas import tpu as pltpu
from jax.sharding import PartitionSpec as P


ROW_TILE = 128
SPAN = 8
EIG = 128
ROWS = 384
SHARE = 16


def moved(value, axis, steps, sends):
    count = lax.axis_size(axis)
    pairs = [(i, i + steps) for i in range(count) if sends(i) and 0 <= i + steps < count]
    return lax.ppermute(value, axis, pairs)


def anyone(line):
    return True


EXCHANGES = {
    "z_up": (5, 4, "sub", -SPAN, anyone),
    "z_down": (4, 5, "sub", SPAN, anyone),
    "x_up": (1, 0, "grp", -1, anyone),
    "y_up": (3, 2, "sub", -1, anyone),
    "y_down": (2, 3, "sub", 1, anyone),
}
ORDER = tuple(EXCHANGES)


def masked(block, tile_count, dim=0):
    index = lax.broadcasted_iota(jnp.int32, block.shape, dim)
    return jnp.where(index < tile_count * ROW_TILE, block, jnp.zeros((), block.dtype))


def contract_rows(left, right):
    return lax.dot_general(
        left, right, (((0,), (0,)), ((), ())), preferred_element_type=jnp.float32
    )


def times(left, right):
    return jnp.dot(left, right, preferred_element_type=jnp.float32)


def shares(block):
    return block.astype(jnp.bfloat16).reshape(EIG // SHARE, SHARE, EIG)


def total(blocks):
    value = blocks[0][...]
    for block in blocks[1:]:
        value = value + block[...]
    return value


def near_kernel(counts, margin, matrices, own_basis, own_image, x_above, out, left):
    for k in range(2, 6):
        product = masked(
            contract_rows(masked(margin[0, k], counts[0, k]), matrices[0, k]), counts[0, k], 1
        )
        high = product.astype(jnp.bfloat16)
        left[2 * (k - 2)] = high
        left[2 * (k - 2) + 1] = (product - high.astype(jnp.float32)).astype(jnp.bfloat16)
    out[:, 0] = shares(contract_rows(own_basis[0], own_image[0]))
    image = times(matrices[0, 0], masked(x_above[...], counts[0, 0])).astype(jnp.bfloat16)
    along_x = contract_rows(masked(margin[0, 0], counts[0, 0]), image)
    out[:, 1] = shares(along_x)
    out[:, 2] = shares(along_x.T)


def far_kernel(left, near, *refs):
    out, received = refs[-1], list(refs[:-1])
    out[:, :3] = near[...]
    for k in range(2, 6):
        parts = [received.pop(0) for e in EXCHANGES.values() if e[1] == k]
        value = total(parts)
        block = times(left[2 * (k - 2)], value)
        if k % 2 == 0:
            block = block + times(left[2 * (k - 2) + 1], value)
        out[:, 1 + k] = shares(block)


def spread_kernel(rows, out):
    out[:, :2] = rows[:, :2].astype(jnp.float32)
    out[0, 2] = jnp.zeros((SHARE, EIG), jnp.float32)
    out[1:, 2] = rows[:-1, 2].astype(jnp.float32)
    out[:, 3:] = rows[:, 3:].astype(jnp.float32)


def on_chip(value):
    return pltpu.with_memory_space_constraint(value, pltpu.VMEM)


def local(margin_basis, pair_matrix, own_basis, own_image, tile_counts):
    smem = pl.BlockSpec(memory_space=pltpu.SMEM)
    vmem = pl.BlockSpec(memory_space=pltpu.VMEM)
    received = {}
    for name, (sent, serves, axis, steps, sends) in EXCHANGES.items():
        received[name] = on_chip(moved(margin_basis[0, sent], axis, steps, sends))
    near, left = pl.pallas_call(
        near_kernel,
        out_shape=(
            pltpu.VMEM((8, 3, SHARE, EIG), jnp.bfloat16),
            pltpu.VMEM((8, EIG, ROWS), jnp.bfloat16),
        ),
        in_specs=[smem] + [vmem] * 5,
        out_specs=(vmem, vmem),
    )(tile_counts, margin_basis, pair_matrix, own_basis, own_image, received["x_up"])
    arrived = [
        received[n] for k in range(2, 6) for n in ORDER if EXCHANGES[n][1] == k
    ]
    coarse = pl.pallas_call(
        far_kernel,
        out_shape=pltpu.VMEM((8, 7, SHARE, EIG), jnp.bfloat16),
        in_specs=[vmem] * (2 + len(arrived)),
        out_specs=vmem,
    )(on_chip(left), on_chip(near), *arrived)
    rows = lax.all_to_all(coarse, "grp", split_axis=0, concat_axis=0, tiled=True)
    return pl.pallas_call(
        spread_kernel,
        out_shape=jax.ShapeDtypeStruct((8, 7, SHARE, EIG), jnp.float32),
        in_specs=[vmem],
        out_specs=vmem,
    )(on_chip(rows))


def solution(mesh):
    return jax.shard_map(
        local,
        mesh=mesh,
        in_specs=(
            P(("sub", "grp"), None, None, None),
            P(("sub", "grp"), None, None, None),
            P(("sub", "grp"), None, None),
            P(("sub", "grp"), None, None),
            P(("sub", "grp"), None),
        ),
        out_specs=P("sub", None, "grp", None),
        check_vma=False,
    )
```

```python
import jax
import jax.numpy as jnp
from jax import lax
from jax.experimental import pallas as pl
from jax.experimental.pallas import tpu as pltpu
from jax.sharding import PartitionSpec as P


ROW_TILE = 128
SPAN = 8
EIG = 128
ROWS = 384
SHARE = 16


def moved(value, axis, steps, sends):
    count = lax.axis_size(axis)
    pairs = [(i, i + steps) for i in range(count) if sends(i) and 0 <= i + steps < count]
    return lax.ppermute(value, axis, pairs)


def anyone(line):
    return True


def far_side(line):
    return line % (2 * SPAN) >= SPAN


def near_side(line):
    return line % (2 * SPAN) < SPAN


def steps_to_start(line):
    return line % (2 * SPAN) == 1


def not_to_start(line):
    return not steps_to_start(line)


EXCHANGES = {
    "z_up_first": (5, 4, "sub", -SPAN, far_side),
    "y_up_start": (3, 2, "sub", -1, steps_to_start),
    "z_down": (4, 5, "sub", SPAN, anyone),
    "z_up_last": (5, 4, "sub", -SPAN, near_side),
    "y_down": (2, 3, "sub", 1, anyone),
    "x_up": (1, 0, "grp", -1, anyone),
    "y_up": (3, 2, "sub", -1, not_to_start),
}
SLOTS = (0, 2, 3, 4, 5)


def masked(block, tile_count, dim=0):
    index = lax.broadcasted_iota(jnp.int32, block.shape, dim)
    return jnp.where(index < tile_count * ROW_TILE, block, jnp.zeros((), block.dtype))


def contract_rows(left, right):
    return lax.dot_general(
        left, right, (((0,), (0,)), ((), ())), preferred_element_type=jnp.float32
    )


def times(left, right):
    return jnp.dot(left, right, preferred_element_type=jnp.float32)


def shares(block):
    return block.astype(jnp.bfloat16).reshape(EIG // SHARE, SHARE, EIG)


def total(blocks):
    value = blocks[0][...]
    for block in blocks[1:]:
        value = value + block[...]
    return value


def near_kernel(counts, margin, matrices, own_basis, own_image, out, left):
    for place, k in enumerate(SLOTS):
        product = masked(
            contract_rows(masked(margin[0, k], counts[0, k]), matrices[0, k]), counts[0, k], 1
        )
        high = product.astype(jnp.bfloat16)
        left[2 * place] = high
        if k % 2 == 0:
            left[2 * place + 1] = (product - high.astype(jnp.float32)).astype(jnp.bfloat16)
    out[...] = shares(contract_rows(own_basis[0], own_image[0]))


def far_kernel(left, near, *refs):
    out, received = refs[-1], list(refs[:-1])
    out[:, 0] = near[...]
    for place, k in enumerate(SLOTS):
        parts = [received.pop(0) for e in EXCHANGES.values() if e[1] == k]
        value = total(parts)
        block = times(left[2 * place], value)
        if k % 2 == 0:
            block = block + times(left[2 * place + 1], value)
        out[:, 1 + k] = shares(block)
        if k == 0:
            out[:, 2] = shares(block.T)


def spread_kernel(rows, out):
    out[:, :2] = rows[:, :2].astype(jnp.float32)
    out[0, 2] = jnp.zeros((SHARE, EIG), jnp.float32)
    out[1:, 2] = rows[:-1, 2].astype(jnp.float32)
    out[:, 3:] = rows[:, 3:].astype(jnp.float32)


def on_chip(value):
    return pltpu.with_memory_space_constraint(value, pltpu.VMEM)


def local(margin_basis, pair_matrix, own_basis, own_image, tile_counts):
    smem = pl.BlockSpec(memory_space=pltpu.SMEM)
    vmem = pl.BlockSpec(memory_space=pltpu.VMEM)
    received = {}
    for name, (sent, serves, axis, steps, sends) in EXCHANGES.items():
        received[name] = on_chip(moved(margin_basis[0, sent], axis, steps, sends))
    near, left = pl.pallas_call(
        near_kernel,
        out_shape=(
            pltpu.VMEM((8, SHARE, EIG), jnp.bfloat16),
            pltpu.VMEM((2 * len(SLOTS), EIG, ROWS), jnp.bfloat16),
        ),
        in_specs=[smem] + [vmem] * 4,
        out_specs=(vmem, vmem),
    )(tile_counts, margin_basis, pair_matrix, own_basis, own_image)
    arrived = [
        received[n] for k in SLOTS for n in EXCHANGES if EXCHANGES[n][1] == k
    ]
    coarse = pl.pallas_call(
        far_kernel,
        out_shape=pltpu.VMEM((8, 7, SHARE, EIG), jnp.bfloat16),
        in_specs=[vmem] * (2 + len(arrived)),
        out_specs=vmem,
    )(on_chip(left), on_chip(near), *arrived)
    rows = lax.all_to_all(coarse, "grp", split_axis=0, concat_axis=0, tiled=True)
    return pl.pallas_call(
        spread_kernel,
        out_shape=jax.ShapeDtypeStruct((8, 7, SHARE, EIG), jnp.float32),
        in_specs=[vmem],
        out_specs=vmem,
    )(on_chip(rows))


def solution(mesh):
    return jax.shard_map(
        local,
        mesh=mesh,
        in_specs=(
            P(("sub", "grp"), None, None, None),
            P(("sub", "grp"), None, None, None),
            P(("sub", "grp"), None, None),
            P(("sub", "grp"), None, None),
            P(("sub", "grp"), None),
        ),
        out_specs=P("sub", None, "grp", None),
        check_vma=False,
    )
```

```python
import jax
import jax.numpy as jnp
from jax import lax
from jax.experimental import pallas as pl
from jax.experimental.pallas import tpu as pltpu
from jax.sharding import PartitionSpec as P


ROW_TILE = 128
SPAN = 8
EIG = 128
ROWS = 384
SHARE = 16


def moved(value, axis, steps, sends):
    count = lax.axis_size(axis)
    pairs = [(i, i + steps) for i in range(count) if sends(i) and 0 <= i + steps < count]
    return lax.ppermute(value, axis, pairs)


def anyone(line):
    return True


def far_side(line):
    return line % (2 * SPAN) >= SPAN


def near_side(line):
    return line % (2 * SPAN) < SPAN


def turns_down(line):
    return line % (2 * SPAN) == 0


def steps_to_start(line):
    return line % (2 * SPAN) == 1


def inner_rest(line):
    return line % (2 * SPAN) > 1


EXCHANGES = {
    "z_up_first": (5, 4, "sub", -SPAN, far_side),
    "y_up_start": (3, 2, "sub", -1, steps_to_start),
    "z_down": (4, 5, "sub", SPAN, anyone),
    "y_up_turn": (3, 2, "sub", -1, turns_down),
    "z_up_last": (5, 4, "sub", -SPAN, near_side),
    "x_up": (1, 0, "grp", -1, anyone),
    "y_down": (2, 3, "sub", 1, anyone),
    "y_up": (3, 2, "sub", -1, inner_rest),
}
SLOTS = (0, 2, 3, 4, 5)


def masked(block, tile_count, dim=0):
    index = lax.broadcasted_iota(jnp.int32, block.shape, dim)
    return jnp.where(index < tile_count * ROW_TILE, block, jnp.zeros((), block.dtype))


def contract_rows(left, right):
    return lax.dot_general(
        left, right, (((0,), (0,)), ((), ())), preferred_element_type=jnp.float32
    )


def times(left, right):
    return jnp.dot(left, right, preferred_element_type=jnp.float32)


def shares(block):
    return block.astype(jnp.bfloat16).reshape(EIG // SHARE, SHARE, EIG)


def total(blocks):
    value = blocks[0][...]
    for block in blocks[1:]:
        value = value + block[...]
    return value


def near_kernel(counts, margin, matrices, own_basis, own_image, out, left):
    for place, k in enumerate(SLOTS):
        product = masked(
            contract_rows(masked(margin[0, k], counts[0, k]), matrices[0, k]), counts[0, k], 1
        )
        high = product.astype(jnp.bfloat16)
        left[2 * place] = high
        if k % 2 == 0:
            left[2 * place + 1] = (product - high.astype(jnp.float32)).astype(jnp.bfloat16)
    out[...] = shares(contract_rows(own_basis[0], own_image[0]))


def far_kernel(left, near, *refs):
    out, received = refs[-1], list(refs[:-1])
    out[:, 0] = near[...]
    for place, k in enumerate(SLOTS):
        parts = [received.pop(0) for e in EXCHANGES.values() if e[1] == k]
        value = total(parts)
        block = times(left[2 * place], value)
        if k % 2 == 0:
            block = block + times(left[2 * place + 1], value)
        out[:, 1 + k] = shares(block)
        if k == 0:
            out[:, 2] = shares(block.T)


def spread_kernel(rows, out):
    out[:, :2] = rows[:, :2].astype(jnp.float32)
    out[0, 2] = jnp.zeros((SHARE, EIG), jnp.float32)
    out[1:, 2] = rows[:-1, 2].astype(jnp.float32)
    out[:, 3:] = rows[:, 3:].astype(jnp.float32)


def on_chip(value):
    return pltpu.with_memory_space_constraint(value, pltpu.VMEM)


def local(margin_basis, pair_matrix, own_basis, own_image, tile_counts):
    smem = pl.BlockSpec(memory_space=pltpu.SMEM)
    vmem = pl.BlockSpec(memory_space=pltpu.VMEM)
    received = {}
    for name, (sent, serves, axis, steps, sends) in EXCHANGES.items():
        received[name] = on_chip(moved(margin_basis[0, sent], axis, steps, sends))
    near, left = pl.pallas_call(
        near_kernel,
        out_shape=(
            pltpu.VMEM((8, SHARE, EIG), jnp.bfloat16),
            pltpu.VMEM((2 * len(SLOTS), EIG, ROWS), jnp.bfloat16),
        ),
        in_specs=[smem] + [vmem] * 4,
        out_specs=(vmem, vmem),
    )(tile_counts, margin_basis, pair_matrix, own_basis, own_image)
    arrived = [
        received[n] for k in SLOTS for n in EXCHANGES if EXCHANGES[n][1] == k
    ]
    coarse = pl.pallas_call(
        far_kernel,
        out_shape=pltpu.VMEM((8, 7, SHARE, EIG), jnp.bfloat16),
        in_specs=[vmem] * (2 + len(arrived)),
        out_specs=vmem,
    )(on_chip(left), on_chip(near), *arrived)
    rows = lax.all_to_all(coarse, "grp", split_axis=0, concat_axis=0, tiled=True)
    return pl.pallas_call(
        spread_kernel,
        out_shape=jax.ShapeDtypeStruct((8, 7, SHARE, EIG), jnp.float32),
        in_specs=[vmem],
        out_specs=vmem,
    )(on_chip(rows))


def solution(mesh):
    return jax.shard_map(
        local,
        mesh=mesh,
        in_specs=(
            P(("sub", "grp"), None, None, None),
            P(("sub", "grp"), None, None, None),
            P(("sub", "grp"), None, None),
            P(("sub", "grp"), None, None),
            P(("sub", "grp"), None),
        ),
        out_specs=P("sub", None, "grp", None),
        check_vma=False,
    )
```
